32 devices in a mesh: long: 8 (over y, x, core), short: 4 (over z).
Axes of the slice: x: 2, y: 2, z: 4, core: 2. Of those that a mesh axis runs over, the one named last changes fastest.
Arguments:
- transition: float32 [64, 384, 384], P(('long', 'short')), may hold values from 0 to 1
- innovation: float32 [64, 384], P(('long', 'short')), may hold values from 20 to 80
- observation: float32 [64, 384], P(('long', 'short')), may hold values from 0.05 to 0.5
- effects: float32 [64, 384, 384], P(('long', 'short')), may hold values from -0.0045 to 0.0045
- prior: float32 [384], replicated, may hold values from 0.5 to 2
- right_side: float32 [64, 384, 128], P(('long', 'short')), may hold values from -3 to 3
- tip_right: float32 [384, 128], replicated, may hold values from -6 to 6
Outputs:
- solution: float32 [64, 384, 128], P(('long', 'short'))
- tip_solution: float32 [384, 128], replicated
The draws below stay inside these ranges and needn't reach their ends.
All inputs are finite; a program needn't handle non-finite values.
Results may differ from the reference program's by a relative error of at most 0.0003.
Values sent between devices are 32-bit elements; how exact they have to be, the bound alone decides.
A program may use at most 256 MiB of HBM per device.

```python
import math
import jax
import jax.numpy as jnp
from jax import lax

B = 384
K = 384
NR = 128
NT = 64


def draw_transition(key, part):
    rate_key, link_key = jax.random.split(jax.random.fold_in(key, 11))
    persistence = jax.random.uniform(rate_key, (NT, B), jnp.float32, 0.9, 0.995)
    ahead_rate = jax.random.uniform(link_key, (NT, B), jnp.float32, 0.05, 0.2)
    behind_rate = jnp.roll(ahead_rate, 1, axis=1)
    identity = jnp.eye(B, dtype=jnp.float32)
    ahead_matrix = jnp.roll(identity, 1, axis=1)
    behind_matrix = ahead_matrix.T
    mixing = (1.0 - ahead_rate - behind_rate)[:, :, None] * identity[None] + ahead_rate[:, :, None] * ahead_matrix[None] + behind_rate[:, :, None] * behind_matrix[None]
    return (persistence[:, :, None] * mixing).astype(jnp.float32)


def draw_effects(key, part):
    common_key, block_key = jax.random.split(jax.random.fold_in(key, 23))
    common_part = 0.0013 * jax.random.normal(common_key, (B, K), jnp.float32)
    block_part = 0.0006 * jax.random.normal(block_key, (NT, B, K), jnp.float32)
    loading = common_part[None] + block_part
    return jnp.clip(loading, -0.0045, 0.0045).astype(jnp.float32)


def level_of(own_key, shape, shards, least, largest):
    loudness, own = 1.0, jax.random.fold_in(own_key, 6)
    for axis_at, shards_of in shards:
        steps = jnp.exp(jax.random.uniform(jax.random.fold_in(own, axis_at), (shards_of,), jnp.float32, least / len(shards), largest / len(shards)))
        loudness = loudness * jnp.repeat(steps, shape[axis_at] // shards_of).reshape([-1 if axis == axis_at else 1 for axis in range(len(shape))])
    return loudness


def scatter_about(key, dims, deviation, bound, shards=(), held_as=jnp.bfloat16):
    values = jax.random.normal(key, dims, jnp.float32) * deviation
    if len(shards) > 0:
        values = level_of(key, dims, shards, -0.22, 0.18) * values
    return jnp.clip(values, min=-bound, max=bound).astype(held_as)


def setup_inputs(seed: int = 0) -> dict:
    arg_keys = jax.random.split(jax.random.key(seed), 8)
    return {
        "transition": draw_transition(jax.random.fold_in(arg_keys[7], 71), 0),
        "innovation": jnp.clip(jnp.exp(math.log(80.0) - 1.3862944 * jax.random.uniform(arg_keys[1], (NT, B), jnp.float32) ** level_of(arg_keys[1], (NT, B), ((0, 32),), -0.2, 0.2)), 20.0, 80.0),
        "observation": jnp.clip(jnp.exp(math.log(0.5) - 2.3025851 * jax.random.uniform(arg_keys[2], (NT, B), jnp.float32) ** level_of(arg_keys[2], (NT, B), ((0, 32),), -0.2, 0.2)), 0.05, 0.5),
        "effects": draw_effects(jax.random.fold_in(arg_keys[7], 71), 0),
        "prior": jnp.clip(jnp.exp(jax.random.uniform(arg_keys[4], (K,), jnp.float32, math.log(0.5), math.log(2.0))), 0.5, 2.0),
        "right_side": scatter_about(arg_keys[5], (NT, B, NR), 0.5, 3.0, ((0, 32),), jnp.float32),
        "tip_right": scatter_about(arg_keys[6], (K, NR), 1.0, 6.0, (), jnp.float32),
    }


HIGHEST = lax.Precision.HIGHEST

def gram_prod(left, right):
    return jnp.einsum('ji,jk->ik', left, right, precision=HIGHEST)

def mat_prod(left, right):
    return jnp.matmul(left, right, precision=HIGHEST)

def solve_lower(factor, values):
    return jax.scipy.linalg.solve_triangular(factor, values, lower=True)

def solve_upper(factor, values):
    return jax.scipy.linalg.solve_triangular(factor, values, lower=True, trans=1)

def reference(transition, innovation, observation, effects, prior, right_side, tip_right):
    block_count, node_width = innovation.shape
    tip_width = prior.shape[0]
    side_count = right_side.shape[2]
    identity = jnp.eye(node_width, dtype=jnp.float32)
    weighted_trans = innovation[:, :, None] * transition
    weighted_effect = innovation[:, :, None] * effects

    def successor(items):
        trans_block, trans_weighted, effect_weighted = items
        return (gram_prod(trans_block, trans_weighted), gram_prod(trans_block, effect_weighted))
    succ_diag, succ_arrow = lax.map(successor, (transition, weighted_trans, weighted_effect))
    zero_square = jnp.zeros((1, node_width, node_width), jnp.float32)
    zero_arrow = jnp.zeros((1, node_width, tip_width), jnp.float32)
    next_diag = jnp.concatenate([succ_diag[1:], zero_square], axis=0)
    next_arrow = jnp.concatenate([succ_arrow[1:], zero_arrow], axis=0)
    keep_mask = jnp.where(jnp.arange(block_count) == 0, 0.0, 1.0).astype(jnp.float32)
    couple = -weighted_trans * keep_mask[:, None, None]
    diag_block = (innovation + observation)[:, :, None] * identity + next_diag
    arrow = -weighted_effect + next_arrow
    tip_block = jnp.diag(prior) + jnp.einsum('tji,tjk->ik', effects, weighted_effect, precision=HIGHEST)
    columns = jnp.concatenate([arrow, right_side], axis=2)

    def forward(carry, items):
        factor_prev, solved_prev, tip_terms = carry
        diag_item, couple_item, column_item = items
        link = solve_lower(factor_prev, couple_item.T)
        factor = jnp.linalg.cholesky(diag_item - gram_prod(link, link))
        solved = solve_lower(factor, column_item - gram_prod(link, solved_prev))
        tip_terms = tip_terms + gram_prod(solved[:, :tip_width], solved)
        return ((factor, solved, tip_terms), (factor, link, solved))
    start = (identity, jnp.zeros((node_width, tip_width + side_count), jnp.float32), jnp.zeros((tip_width, tip_width + side_count), jnp.float32))
    final_carry, stored = lax.scan(forward, start, (diag_block, couple, columns))
    tip_terms = final_carry[2]
    factors, links, solved_all = stored
    tip_factor = jnp.linalg.cholesky(tip_block - tip_terms[:, :tip_width])
    tip_solution = solve_upper(tip_factor, solve_lower(tip_factor, tip_right - tip_terms[:, tip_width:]))
    next_links = jnp.concatenate([links[1:], zero_square], axis=0)

    def backward(later, items):
        factor, link_next, solved = items
        value = solved[:, tip_width:] - mat_prod(solved[:, :tip_width], tip_solution) - mat_prod(link_next, later)
        current = solve_upper(factor, value)
        return (current, current)
    last_value, solution = lax.scan(backward, jnp.zeros((node_width, side_count), jnp.float32), (factors, next_links, solved_all), reverse=True)
    return (solution, tip_solution)
```

```python
import jax
import jax.numpy as jnp
from jax import lax
from jax.experimental import pallas as pl
from jax.experimental.pallas import tpu as pltpu
from jax.sharding import PartitionSpec as P

AXES = ("long", "short")
PREC = lax.Precision.HIGHEST
LANES = 128
SUBLANES = 8


def gram_prod(left, right):
    return jnp.einsum("ji,jk->ik", left, right, precision=PREC)


def mat_prod(left, right):
    return jnp.matmul(left, right, precision=PREC)


def pivot_pair(tiles, first, lane, sub):
    group, row = divmod(first, SUBLANES)
    shape = (SUBLANES, LANES)
    col0 = [jnp.broadcast_to(t[:, first : first + 1], shape) for t in tiles]
    col1 = [jnp.broadcast_to(t[:, first + 1 : first + 2], shape) for t in tiles]
    at0, at1 = lane == first, lane == first + 1
    a = col0[group][row : row + 1, :]
    b = col1[group][row : row + 1, :]
    c = col1[group][row + 1 : row + 2, :]
    inv = 1.0 / (a * c - b * b)
    row0 = tiles[group][row : row + 1, :]
    row1 = tiles[group][row + 1 : row + 2, :]
    at0_row, at1_row = at0[:1], at1[:1]
    row0 = jnp.where(at0_row, 1.0, jnp.where(at1_row, 0.0, row0))
    row1 = jnp.where(at1_row, 1.0, jnp.where(at0_row, 0.0, row1))
    q0 = jnp.broadcast_to((c * row0 - b * row1) * inv, shape)
    q1 = jnp.broadcast_to((a * row1 - b * row0) * inv, shape)
    both = jnp.logical_or(at0, at1)
    out = []
    for place, tile in enumerate(tiles):
        new = jnp.where(both, 0.0, tile) - col0[place] * q0 - col1[place] * q1
        if place == group:
            new = jnp.where(sub == row, q0, jnp.where(sub == row + 1, q1, new))
        out.append(new)
    return out


def inverse_kernel(a_ref, o_ref):
    width = a_ref.shape[0]
    lane = lax.broadcasted_iota(jnp.int32, (SUBLANES, LANES), 1)
    sub = lax.broadcasted_iota(jnp.int32, (SUBLANES, LANES), 0)
    o_ref[...] = a_ref[...]

    def step(k, carry):
        at = pl.multiple_of(k * LANES, LANES)
        here = pl.ds(at, LANES)
        tiles = [
            o_ref[pl.ds(pl.multiple_of(at + SUBLANES * g, SUBLANES), SUBLANES), here]
            for g in range(LANES // SUBLANES)
        ]
        for first in range(0, LANES, 2):
            tiles = pivot_pair(tiles, first, lane, sub)
        pivot = jnp.concatenate(tiles, axis=0)
        rows = o_ref[here, :]
        columns = o_ref[:, here]
        scaled = jnp.dot(pivot, rows, precision=PREC, preferred_element_type=jnp.float32)
        o_ref[here, :] = scaled
        o_ref[here, here] = pivot
        scaled = o_ref[here, :]
        o_ref[:, here] = jnp.zeros((width, LANES), jnp.float32)
        o_ref[...] = o_ref[...] - jnp.dot(
            columns, scaled, precision=PREC, preferred_element_type=jnp.float32
        )
        o_ref[here, :] = scaled
        return carry

    lax.fori_loop(0, width // LANES, step, 0)


def spd_inverse(matrix):
    width = matrix.shape[0]
    return pl.pallas_call(
        inverse_kernel,
        out_shape=jax.ShapeDtypeStruct(matrix.shape, jnp.float32),
        in_specs=[pl.BlockSpec(memory_space=pltpu.VMEM)],
        out_specs=pl.BlockSpec(memory_space=pltpu.VMEM),
        cost_estimate=pl.CostEstimate(
            flops=300 * width**3, bytes_accessed=8 * width**2, transcendentals=0
        ),
        name="spd_inverse",
    )(matrix)


def body(transition, innovation, observation, effects, prior, right_side, tip_right):
    block_count, node_width = innovation.shape
    tip_width = prior.shape[0]
    total = lax.axis_size(AXES)
    position = lax.axis_index(AXES)
    identity = jnp.eye(node_width, dtype=jnp.float32)

    def send(values, pairs):
        return lax.ppermute(values, AXES, pairs)

    weighted_trans = innovation[:, :, None] * transition
    weighted_effect = innovation[:, :, None] * effects
    succ_diag = [gram_prod(transition[t], weighted_trans[t]) for t in range(block_count)]
    succ_arrow = [gram_prod(transition[t], weighted_effect[t]) for t in range(block_count)]
    tip_terms = gram_prod(
        effects.reshape(-1, tip_width), weighted_effect.reshape(-1, tip_width)
    )
    global_block = position * block_count + jnp.arange(block_count)
    couple = -weighted_trans * jnp.where(global_block == 0, 0.0, 1.0)[:, None, None]
    diag_base = (innovation + observation)[:, :, None] * identity
    interior = block_count - 1

    stored = []
    left_diag = left_arrow = left_rhs = 0.0
    diag_item = arrow_item = rhs_item = left_item = None
    for t in range(block_count):
        if t == 0:
            diag_item = diag_base[t]
            arrow_item = -weighted_effect[t]
            rhs_item = right_side[t]
            left_item = couple[t]
        else:
            _, link, y_left, y_arrow, y_rhs = stored[-1]
            diag_item = diag_base[t] - mat_prod(couple[t], link)
            arrow_item = -weighted_effect[t] - mat_prod(couple[t], y_arrow)
            rhs_item = right_side[t] - mat_prod(couple[t], y_rhs)
            left_item = -mat_prod(couple[t], y_left)
        if t < interior:
            diag_item = diag_item + succ_diag[t + 1]
            arrow_item = arrow_item + succ_arrow[t + 1]
            inverse = spd_inverse(diag_item)
            link = jnp.einsum("ij,kj->ik", inverse, couple[t + 1], precision=PREC)
            y_left = mat_prod(inverse, left_item)
            y_arrow = mat_prod(inverse, arrow_item)
            y_rhs = mat_prod(inverse, rhs_item)
            left_diag = left_diag - gram_prod(left_item, y_left)
            left_arrow = left_arrow - gram_prod(left_item, y_arrow)
            left_rhs = left_rhs - gram_prod(left_item, y_rhs)
            tip_terms = tip_terms - gram_prod(arrow_item, y_arrow)
            tip_part = gram_prod(arrow_item, y_rhs)
            tip_rhs_terms = -tip_part if t == 0 else tip_rhs_terms - tip_part
            stored.append((inverse, link, y_left, y_arrow, y_rhs))
    if interior == 0:
        tip_rhs_terms = jnp.zeros_like(tip_right)

    to_left = [(i, i - 1) for i in range(1, total)]
    node_diag = diag_item + send(left_diag + succ_diag[0], to_left)
    node_arrow = arrow_item + send(left_arrow + succ_arrow[0], to_left)
    node_rhs = rhs_item
    if interior > 0:
        node_rhs = node_rhs + send(left_rhs, to_left)
    node_couple = left_item

    levels = []
    distance = 1
    while distance < total:
        d = distance
        drops = [i for i in range(total) if (i + 1) % d == 0 and (i + 1) // d % 2 == 1]
        rightward = [(i, i + d) for i in drops if i + d < total]
        leftward = [(i, i - d) for i in drops if i >= d]
        back_right = [(j, i) for i, j in rightward]
        back_left = [(j, i) for i, j in leftward]
        rank = position + 1
        drop = jnp.logical_and(rank % d == 0, rank // d % 2 == 1)
        fed = jnp.logical_and(rank % (2 * d) == 0, position >= d)
        right_item = send(node_couple, back_right).T
        inverse = spd_inverse(node_diag)
        y_right = mat_prod(inverse, right_item)
        y_left = mat_prod(inverse, node_couple)
        diag_right = send(gram_prod(right_item, y_right), rightward)
        diag_left = send(gram_prod(node_couple, y_left), leftward)
        y_arrow = mat_prod(inverse, node_arrow)
        y_rhs = mat_prod(inverse, node_rhs)
        new_couple = send(gram_prod(right_item, y_left), rightward)
        arrow_right = send(gram_prod(right_item, y_arrow), rightward)
        arrow_left = send(gram_prod(node_couple, y_arrow), leftward)
        rhs_right = send(gram_prod(right_item, y_rhs), rightward)
        rhs_left = send(gram_prod(node_couple, y_rhs), leftward)
        tip_terms = tip_terms - jnp.where(drop, gram_prod(node_arrow, y_arrow), 0.0)
        tip_rhs_terms = tip_rhs_terms - jnp.where(drop, gram_prod(node_arrow, y_rhs), 0.0)
        levels.append((drop, back_left, back_right, y_left, y_right, y_arrow, y_rhs))
        node_diag = node_diag - diag_right - diag_left
        node_couple = jnp.where(fed, -new_couple, node_couple)
        node_arrow = node_arrow - arrow_right - arrow_left
        node_rhs = node_rhs - rhs_right - rhs_left
        distance *= 2

    final = position == total - 1
    inverse = spd_inverse(node_diag)
    y_arrow = mat_prod(inverse, node_arrow)
    y_rhs = mat_prod(inverse, node_rhs)
    tip_terms = tip_terms - jnp.where(final, gram_prod(node_arrow, y_arrow), 0.0)
    tip_rhs_terms = tip_rhs_terms - jnp.where(final, gram_prod(node_arrow, y_rhs), 0.0)
    tip_total, tip_rhs_total = lax.psum((tip_terms, tip_rhs_terms), AXES)
    tip_solution = mat_prod(spd_inverse(tip_total + jnp.diag(prior)), tip_rhs_total + tip_right)

    node_x = y_rhs - mat_prod(y_arrow, tip_solution)
    for drop, back_left, back_right, y_left, y_right, y_arrow, y_rhs in reversed(levels):
        base = y_rhs - mat_prod(y_arrow, tip_solution)
        left_x = send(node_x, back_left)
        right_x = send(node_x, back_right)
        value = base - mat_prod(y_left, left_x) - mat_prod(y_right, right_x)
        node_x = jnp.where(drop, value, node_x)
    left_x = send(node_x, [(i, i + 1) for i in range(total - 1)])
    outs = [node_x]
    for inverse, link, y_left, y_arrow, y_rhs in reversed(stored):
        value = (
            y_rhs
            - mat_prod(y_arrow, tip_solution)
            - mat_prod(y_left, left_x)
            - mat_prod(link, outs[0])
        )
        outs.insert(0, value)
    return (jnp.stack(outs, axis=0), tip_solution)


def solution(mesh):
    placed = (
        P(AXES, None, None),
        P(AXES, None),
        P(AXES, None),
        P(AXES, None, None),
        P(),
        P(AXES, None, None),
        P(),
    )
    return jax.shard_map(
        body,
        mesh=mesh,
        in_specs=placed,
        out_specs=(P(AXES, None, None), P()),
        check_vma=False,
    )
```

```python
import jax
import jax.numpy as jnp
from jax import lax
from jax.experimental import pallas as pl
from jax.experimental.pallas import tpu as pltpu
from jax.sharding import PartitionSpec as P

AXES = ("long", "short")
PREC = lax.Precision.HIGHEST
FAST = lax.Precision.HIGHEST
LANES = 128
SUBLANES = 8


def gram_prod(left, right, precision=FAST):
    return jnp.einsum("ji,jk->ik", left, right, precision=precision)


def mat_prod(left, right, precision=FAST):
    return jnp.matmul(left, right, precision=precision)


def inverse_two(a, b, c):
    inv = 1.0 / (a * c - b * b)
    return c * inv, -(b * inv), a * inv


def pivot_four(tiles, first, lane, sub):
    group, row = divmod(first, SUBLANES)
    shape = (SUBLANES, LANES)
    cols = [
        [jnp.broadcast_to(t[:, first + k : first + k + 1], shape) for t in tiles] for k in range(4)
    ]

    def entry(i, k):
        return cols[k][group][row + i : row + i + 1, :]

    a00, a01, a11 = inverse_two(entry(0, 0), entry(0, 1), entry(1, 1))
    b00, b01, b10, b11 = entry(0, 2), entry(0, 3), entry(1, 2), entry(1, 3)
    m00, m01 = a00 * b00 + a01 * b10, a00 * b01 + a01 * b11
    m10, m11 = a01 * b00 + a11 * b10, a01 * b01 + a11 * b11
    s00, s01, s11 = inverse_two(
        entry(2, 2) - (b00 * m00 + b10 * m10),
        entry(2, 3) - (b00 * m01 + b10 * m11),
        entry(3, 3) - (b01 * m01 + b11 * m11),
    )
    u00, u01 = m00 * s00 + m01 * s01, m00 * s01 + m01 * s11
    u10, u11 = m10 * s00 + m11 * s01, m10 * s01 + m11 * s11
    t01 = a01 + (u00 * m10 + u01 * m11)
    pivot_inverse = (
        (a00 + (u00 * m00 + u01 * m01), t01, -u00, -u01),
        (t01, a11 + (u10 * m10 + u11 * m11), -u10, -u11),
        (-u00, -u10, s00, s01),
        (-u01, -u11, s01, s11),
    )
    inside = jnp.logical_and(lane >= first, lane < first + 4)
    rows = [
        jnp.where(
            inside[:1],
            jnp.where(lane[:1] == first + k, 1.0, 0.0),
            tiles[group][row + k : row + k + 1, :],
        )
        for k in range(4)
    ]
    scaled = [
        jnp.broadcast_to(
            (p[0] * rows[0] + p[1] * rows[1]) + (p[2] * rows[2] + p[3] * rows[3]), shape
        )
        for p in pivot_inverse
    ]
    out = []
    for place, tile in enumerate(tiles):
        new = jnp.where(inside, 0.0, tile)
        for k in range(4):
            new = new - cols[k][place] * scaled[k]
        if place == group:
            for k in range(4):
                new = jnp.where(sub == row + k, scaled[k], new)
        out.append(new)
    return out


def inverse_kernel(a_ref, o_ref):
    width = a_ref.shape[0]
    lane = lax.broadcasted_iota(jnp.int32, (SUBLANES, LANES), 1)
    sub = lax.broadcasted_iota(jnp.int32, (SUBLANES, LANES), 0)
    o_ref[...] = a_ref[...]

    def step(k, carry):
        at = pl.multiple_of(k * LANES, LANES)
        here = pl.ds(at, LANES)
        tiles = [
            o_ref[pl.ds(pl.multiple_of(at + SUBLANES * g, SUBLANES), SUBLANES), here]
            for g in range(LANES // SUBLANES)
        ]
        for first in range(0, LANES, 4):
            tiles = pivot_four(tiles, first, lane, sub)
        pivot = jnp.concatenate(tiles, axis=0)
        rows = o_ref[here, :]
        columns = o_ref[:, here]
        scaled = jnp.dot(pivot, rows, precision=PREC, preferred_element_type=jnp.float32)
        o_ref[here, :] = scaled
        o_ref[here, here] = pivot
        scaled = o_ref[here, :]
        o_ref[:, here] = jnp.zeros((width, LANES), jnp.float32)
        o_ref[...] = o_ref[...] - jnp.dot(
            columns, scaled, precision=PREC, preferred_element_type=jnp.float32
        )
        o_ref[here, :] = scaled
        return carry

    lax.fori_loop(0, width // LANES, step, 0)


def spd_inverse(matrix):
    width = matrix.shape[0]
    return pl.pallas_call(
        inverse_kernel,
        out_shape=jax.ShapeDtypeStruct(matrix.shape, jnp.float32),
        in_specs=[pl.BlockSpec(memory_space=pltpu.VMEM)],
        out_specs=pl.BlockSpec(memory_space=pltpu.VMEM),
        cost_estimate=pl.CostEstimate(
            flops=300 * width**3, bytes_accessed=8 * width**2, transcendentals=0
        ),
        name="spd_inverse",
    )(matrix)


def body(transition, innovation, observation, effects, prior, right_side, tip_right):
    block_count, node_width = innovation.shape
    tip_width = prior.shape[0]
    total = lax.axis_size(AXES)
    position = lax.axis_index(AXES)
    identity = jnp.eye(node_width, dtype=jnp.float32)

    def send(values, pairs):
        return lax.ppermute(values, AXES, pairs)

    weighted_trans = innovation[:, :, None] * transition
    weighted_effect = innovation[:, :, None] * effects
    succ_diag = [gram_prod(transition[t], weighted_trans[t], PREC) for t in range(block_count)]
    succ_arrow = [gram_prod(transition[t], weighted_effect[t], PREC) for t in range(block_count)]
    tip_terms = gram_prod(
        effects.reshape(-1, tip_width), weighted_effect.reshape(-1, tip_width), PREC
    )
    global_block = position * block_count + jnp.arange(block_count)
    couple = -weighted_trans * jnp.where(global_block == 0, 0.0, 1.0)[:, None, None]
    diag_base = (innovation + observation)[:, :, None] * identity
    interior = block_count - 1

    stored = []
    left_diag = left_arrow = left_rhs = 0.0
    diag_item = arrow_item = rhs_item = left_item = None
    for t in range(block_count):
        if t == 0:
            diag_item = diag_base[t]
            arrow_item = -weighted_effect[t]
            rhs_item = right_side[t]
            left_item = couple[t]
        else:
            _, link, y_left, y_arrow, y_rhs = stored[-1]
            diag_item = diag_base[t] - mat_prod(couple[t], link)
            arrow_item = -weighted_effect[t] - mat_prod(couple[t], y_arrow)
            rhs_item = right_side[t] - mat_prod(couple[t], y_rhs)
            left_item = -mat_prod(couple[t], y_left)
        if t < interior:
            diag_item = diag_item + succ_diag[t + 1]
            arrow_item = arrow_item + succ_arrow[t + 1]
            inverse = spd_inverse(diag_item)
            link = jnp.einsum("ij,kj->ik", inverse, couple[t + 1], precision=FAST)
            y_left = mat_prod(inverse, left_item)
            y_arrow = mat_prod(inverse, arrow_item)
            y_rhs = mat_prod(inverse, rhs_item)
            left_diag = left_diag - gram_prod(left_item, y_left)
            left_arrow = left_arrow - gram_prod(left_item, y_arrow)
            left_rhs = left_rhs - gram_prod(left_item, y_rhs)
            tip_terms = tip_terms - gram_prod(arrow_item, y_arrow)
            tip_part = gram_prod(arrow_item, y_rhs)
            tip_rhs_terms = -tip_part if t == 0 else tip_rhs_terms - tip_part
            stored.append((inverse, link, y_left, y_arrow, y_rhs))
    if interior == 0:
        tip_rhs_terms = jnp.zeros_like(tip_right)

    to_left = [(i, i - 1) for i in range(1, total)]
    node_diag = diag_item + send(left_diag + succ_diag[0], to_left)
    node_arrow = arrow_item + send(left_arrow + succ_arrow[0], to_left)
    node_rhs = rhs_item
    if interior > 0:
        node_rhs = node_rhs + send(left_rhs, to_left)
    node_couple = left_item

    levels = []
    distance = 1
    while distance < total:
        d = distance
        drops = [i for i in range(total) if (i + 1) % d == 0 and (i + 1) // d % 2 == 1]
        rightward = [(i, i + d) for i in drops if i + d < total]
        leftward = [(i, i - d) for i in drops if i >= d]
        back_right = [(j, i) for i, j in rightward]
        back_left = [(j, i) for i, j in leftward]
        rank = position + 1
        drop = jnp.logical_and(rank % d == 0, rank // d % 2 == 1)
        fed = jnp.logical_and(rank % (2 * d) == 0, position >= d)
        right_item = send(node_couple, back_right).T
        inverse = spd_inverse(node_diag)
        y_right = mat_prod(inverse, right_item)
        y_left = mat_prod(inverse, node_couple)
        diag_right = send(gram_prod(right_item, y_right), rightward)
        diag_left = send(gram_prod(node_couple, y_left), leftward)
        y_arrow = mat_prod(inverse, node_arrow)
        y_rhs = mat_prod(inverse, node_rhs)
        new_couple = send(gram_prod(right_item, y_left), rightward)
        arrow_right = send(gram_prod(right_item, y_arrow), rightward)
        arrow_left = send(gram_prod(node_couple, y_arrow), leftward)
        rhs_right = send(gram_prod(right_item, y_rhs), rightward)
        rhs_left = send(gram_prod(node_couple, y_rhs), leftward)
        tip_passed = send(tip_terms - gram_prod(node_arrow, y_arrow), rightward)
        tip_rhs_passed = send(tip_rhs_terms - gram_prod(node_arrow, y_rhs), rightward)
        tip_terms = tip_terms + tip_passed
        tip_rhs_terms = tip_rhs_terms + tip_rhs_passed
        levels.append((drop, back_left, back_right, y_left, y_right, y_arrow, y_rhs))
        node_diag = node_diag - diag_right - diag_left
        node_couple = jnp.where(fed, -new_couple, node_couple)
        node_arrow = node_arrow - arrow_right - arrow_left
        node_rhs = node_rhs - rhs_right - rhs_left
        distance *= 2

    final = position == total - 1
    inverse = spd_inverse(node_diag)
    y_arrow = mat_prod(inverse, node_arrow)
    y_rhs = mat_prod(inverse, node_rhs)
    tip_total = tip_terms - gram_prod(node_arrow, y_arrow) + jnp.diag(prior)
    tip_rhs_total = tip_rhs_terms - gram_prod(node_arrow, y_rhs) + tip_right
    tip_found = mat_prod(spd_inverse(tip_total), tip_rhs_total)
    tip_solution = jnp.where(final, tip_found, 0.0)
    node_x = jnp.where(final, y_rhs - mat_prod(y_arrow, tip_solution), 0.0)

    for drop, back_left, back_right, y_left, y_right, y_arrow, y_rhs in reversed(levels):
        tip_solution = tip_solution + send(tip_solution, back_right)
        left_x = send(node_x, back_left)
        right_x = send(node_x, back_right)
        value = (
            y_rhs
            - mat_prod(y_arrow, tip_solution)
            - mat_prod(y_left, left_x)
            - mat_prod(y_right, right_x)
        )
        node_x = jnp.where(drop, value, node_x)
    left_x = send(node_x, [(i, i + 1) for i in range(total - 1)])
    outs = [node_x]
    for inverse, link, y_left, y_arrow, y_rhs in reversed(stored):
        value = (
            y_rhs
            - mat_prod(y_arrow, tip_solution)
            - mat_prod(y_left, left_x)
            - mat_prod(link, outs[0])
        )
        outs.insert(0, value)
    return (jnp.stack(outs, axis=0), tip_solution)


def solution(mesh):
    placed = (
        P(AXES, None, None),
        P(AXES, None),
        P(AXES, None),
        P(AXES, None, None),
        P(),
        P(AXES, None, None),
        P(),
    )
    return jax.shard_map(
        body,
        mesh=mesh,
        in_specs=placed,
        out_specs=(P(AXES, None, None), P()),
        check_vma=False,
    )
```

```python
import jax
import jax.numpy as jnp
from jax import lax
from jax.experimental import pallas as pl
from jax.experimental.pallas import tpu as pltpu
from jax.sharding import PartitionSpec as P

AXES = ("long", "short")
PREC = lax.Precision.HIGHEST
FAST = lax.Precision.HIGHEST
LANES = 128
SUBLANES = 8


def gram_prod(left, right, precision=FAST):
    return jnp.einsum("ji,jk->ik", left, right, precision=precision)


def mat_prod(left, right, precision=FAST):
    return jnp.matmul(left, right, precision=precision)


def inverse_two(a, b, c):
    inv = 1.0 / (a * c - b * b)
    return c * inv, -(b * inv), a * inv


def pivot_four(tiles, first, lane, sub):
    group, row = divmod(first, SUBLANES)
    shape = (SUBLANES, LANES)
    cols = [
        [jnp.broadcast_to(t[:, first + k : first + k + 1], shape) for t in tiles] for k in range(4)
    ]

    def entry(i, k):
        return cols[k][group][row + i : row + i + 1, :]

    a00, a01, a11 = inverse_two(entry(0, 0), entry(0, 1), entry(1, 1))
    b00, b01, b10, b11 = entry(0, 2), entry(0, 3), entry(1, 2), entry(1, 3)
    m00, m01 = a00 * b00 + a01 * b10, a00 * b01 + a01 * b11
    m10, m11 = a01 * b00 + a11 * b10, a01 * b01 + a11 * b11
    s00, s01, s11 = inverse_two(
        entry(2, 2) - (b00 * m00 + b10 * m10),
        entry(2, 3) - (b00 * m01 + b10 * m11),
        entry(3, 3) - (b01 * m01 + b11 * m11),
    )
    u00, u01 = m00 * s00 + m01 * s01, m00 * s01 + m01 * s11
    u10, u11 = m10 * s00 + m11 * s01, m10 * s01 + m11 * s11
    t01 = a01 + (u00 * m10 + u01 * m11)
    pivot_inverse = (
        (a00 + (u00 * m00 + u01 * m01), t01, -u00, -u01),
        (t01, a11 + (u10 * m10 + u11 * m11), -u10, -u11),
        (-u00, -u10, s00, s01),
        (-u01, -u11, s01, s11),
    )
    inside = jnp.logical_and(lane >= first, lane < first + 4)
    rows = [
        jnp.where(
            inside[:1],
            jnp.where(lane[:1] == first + k, 1.0, 0.0),
            tiles[group][row + k : row + k + 1, :],
        )
        for k in range(4)
    ]
    scaled = [
        jnp.broadcast_to(
            (p[0] * rows[0] + p[1] * rows[1]) + (p[2] * rows[2] + p[3] * rows[3]), shape
        )
        for p in pivot_inverse
    ]
    out = []
    for place, tile in enumerate(tiles):
        new = jnp.where(inside, 0.0, tile)
        for k in range(4):
            new = new - cols[k][place] * scaled[k]
        if place == group:
            for k in range(4):
                new = jnp.where(sub == row + k, scaled[k], new)
        out.append(new)
    return out


def inverse_kernel(a_ref, o_ref):
    width = a_ref.shape[0]
    lane = lax.broadcasted_iota(jnp.int32, (SUBLANES, LANES), 1)
    sub = lax.broadcasted_iota(jnp.int32, (SUBLANES, LANES), 0)
    o_ref[...] = a_ref[...]

    def step(k, carry):
        at = pl.multiple_of(k * LANES, LANES)
        here = pl.ds(at, LANES)
        tiles = [
            o_ref[pl.ds(pl.multiple_of(at + SUBLANES * g, SUBLANES), SUBLANES), here]
            for g in range(LANES // SUBLANES)
        ]
        for first in range(0, LANES, 4):
            tiles = pivot_four(tiles, first, lane, sub)
        pivot = jnp.concatenate(tiles, axis=0)
        rows = o_ref[here, :]
        columns = o_ref[:, here]
        scaled = jnp.dot(pivot, rows, precision=PREC, preferred_element_type=jnp.float32)
        o_ref[here, :] = scaled
        o_ref[here, here] = pivot
        scaled = o_ref[here, :]
        o_ref[:, here] = jnp.zeros((width, LANES), jnp.float32)
        o_ref[...] = o_ref[...] - jnp.dot(
            columns, scaled, precision=PREC, preferred_element_type=jnp.float32
        )
        o_ref[here, :] = scaled
        return carry

    lax.fori_loop(0, width // LANES, step, 0)


def spd_inverse(matrix):
    width = matrix.shape[0]
    return pl.pallas_call(
        inverse_kernel,
        out_shape=jax.ShapeDtypeStruct(matrix.shape, jnp.float32),
        in_specs=[pl.BlockSpec(memory_space=pltpu.VMEM)],
        out_specs=pl.BlockSpec(memory_space=pltpu.VMEM),
        cost_estimate=pl.CostEstimate(
            flops=300 * width**3, bytes_accessed=8 * width**2, transcendentals=0
        ),
        name="spd_inverse",
    )(matrix)


def body(transition, innovation, observation, effects, prior, right_side, tip_right):
    block_count, node_width = innovation.shape
    tip_width = prior.shape[0]
    total = lax.axis_size(AXES)
    position = lax.axis_index(AXES)
    identity = jnp.eye(node_width, dtype=jnp.float32)

    def send(values, pairs):
        return lax.ppermute(values, AXES, pairs)

    weighted_trans = innovation[:, :, None] * transition
    weighted_effect = innovation[:, :, None] * effects
    succ_diag = [gram_prod(transition[t], weighted_trans[t], PREC) for t in range(block_count)]
    succ_arrow = [gram_prod(transition[t], weighted_effect[t], PREC) for t in range(block_count)]
    tip_terms = gram_prod(
        effects.reshape(-1, tip_width), weighted_effect.reshape(-1, tip_width), PREC
    )
    global_block = position * block_count + jnp.arange(block_count)
    couple = -weighted_trans * jnp.where(global_block == 0, 0.0, 1.0)[:, None, None]
    diag_base = (innovation + observation)[:, :, None] * identity
    interior = block_count - 1

    stored = []
    left_diag = left_arrow = left_rhs = 0.0
    diag_item = arrow_item = rhs_item = left_item = None
    for t in range(block_count):
        if t == 0:
            diag_item = diag_base[t]
            arrow_item = -weighted_effect[t]
            rhs_item = right_side[t]
            left_item = couple[t]
        else:
            _, link, y_left, y_arrow, y_rhs = stored[-1]
            diag_item = diag_base[t] - mat_prod(couple[t], link)
            arrow_item = -weighted_effect[t] - mat_prod(couple[t], y_arrow)
            rhs_item = right_side[t] - mat_prod(couple[t], y_rhs)
            left_item = -mat_prod(couple[t], y_left)
        if t < interior:
            diag_item = diag_item + succ_diag[t + 1]
            arrow_item = arrow_item + succ_arrow[t + 1]
            inverse = spd_inverse(diag_item)
            link = jnp.einsum("ij,kj->ik", inverse, couple[t + 1], precision=FAST)
            y_left = mat_prod(inverse, left_item)
            y_arrow = mat_prod(inverse, arrow_item)
            y_rhs = mat_prod(inverse, rhs_item)
            left_diag = left_diag - gram_prod(left_item, y_left)
            left_arrow = left_arrow - gram_prod(left_item, y_arrow)
            left_rhs = left_rhs - gram_prod(left_item, y_rhs)
            tip_terms = tip_terms - gram_prod(arrow_item, y_arrow)
            tip_part = gram_prod(arrow_item, y_rhs)
            tip_rhs_terms = -tip_part if t == 0 else tip_rhs_terms - tip_part
            stored.append((inverse, link, y_left, y_arrow, y_rhs))
    if interior == 0:
        tip_rhs_terms = jnp.zeros_like(tip_right)

    to_left = [(i, i - 1) for i in range(1, total)]
    node_diag = diag_item + send(left_diag + succ_diag[0], to_left)
    node_arrow = arrow_item + send(left_arrow + succ_arrow[0], to_left)
    node_rhs = rhs_item
    if interior > 0:
        node_rhs = node_rhs + send(left_rhs, to_left)
    node_couple = left_item

    levels = []
    distance = 1
    while distance < total:
        d = distance
        drops = [i for i in range(total) if (i + 1) % d == 0 and (i + 1) // d % 2 == 1]
        rightward = [(i, i + d) for i in drops if i + d < total]
        leftward = [(i, i - d) for i in drops if i >= d]
        back_right = [(j, i) for i, j in rightward]
        back_left = [(j, i) for i, j in leftward]
        rank = position + 1
        drop = jnp.logical_and(rank % d == 0, rank // d % 2 == 1)
        fed = jnp.logical_and(rank % (2 * d) == 0, position >= d)
        right_item = send(node_couple, back_right).T
        inverse = spd_inverse(node_diag)
        y_right = mat_prod(inverse, right_item)
        y_left = mat_prod(inverse, node_couple)
        diag_right, diag_left, inverse = lax.optimization_barrier(
            (gram_prod(right_item, y_right), gram_prod(node_couple, y_left), inverse)
        )
        diag_right = send(diag_right, rightward)
        diag_left = send(diag_left, leftward)
        y_arrow = mat_prod(inverse, node_arrow)
        y_rhs = mat_prod(inverse, node_rhs)
        new_couple = send(gram_prod(right_item, y_left), rightward)
        arrow_right = send(gram_prod(right_item, y_arrow), rightward)
        arrow_left = send(gram_prod(node_couple, y_arrow), leftward)
        rhs_right = send(gram_prod(right_item, y_rhs), rightward)
        rhs_left = send(gram_prod(node_couple, y_rhs), leftward)
        tip_passed = send(tip_terms - gram_prod(node_arrow, y_arrow), rightward)
        tip_rhs_passed = send(tip_rhs_terms - gram_prod(node_arrow, y_rhs), rightward)
        tip_terms = tip_terms + tip_passed
        tip_rhs_terms = tip_rhs_terms + tip_rhs_passed
        levels.append((drop, back_left, back_right, y_left, y_right, y_arrow, y_rhs))
        node_diag = node_diag - diag_right - diag_left
        node_couple = jnp.where(fed, -new_couple, node_couple)
        node_arrow = node_arrow - arrow_right - arrow_left
        node_rhs = node_rhs - rhs_right - rhs_left
        distance *= 2

    final = position == total - 1
    inverse = spd_inverse(node_diag)
    y_arrow = mat_prod(inverse, node_arrow)
    y_rhs = mat_prod(inverse, node_rhs)
    tip_total = tip_terms - gram_prod(node_arrow, y_arrow) + jnp.diag(prior)
    tip_rhs_total = tip_rhs_terms - gram_prod(node_arrow, y_rhs) + tip_right
    tip_found = mat_prod(spd_inverse(tip_total), tip_rhs_total)
    tip_solution = jnp.where(final, tip_found, 0.0)
    node_x = jnp.where(final, y_rhs - mat_prod(y_arrow, tip_solution), 0.0)

    for drop, back_left, back_right, y_left, y_right, y_arrow, y_rhs in reversed(levels):
        tip_solution = tip_solution + send(tip_solution, back_right)
        left_x = send(node_x, back_left)
        right_x = send(node_x, back_right)
        value = (
            y_rhs
            - mat_prod(y_arrow, tip_solution)
            - mat_prod(y_left, left_x)
            - mat_prod(y_right, right_x)
        )
        node_x = jnp.where(drop, value, node_x)
    left_x = send(node_x, [(i, i + 1) for i in range(total - 1)])
    outs = [node_x]
    for inverse, link, y_left, y_arrow, y_rhs in reversed(stored):
        value = (
            y_rhs
            - mat_prod(y_arrow, tip_solution)
            - mat_prod(y_left, left_x)
            - mat_prod(link, outs[0])
        )
        outs.insert(0, value)
    return (jnp.stack(outs, axis=0), tip_solution)


def solution(mesh):
    placed = (
        P(AXES, None, None),
        P(AXES, None),
        P(AXES, None),
        P(AXES, None, None),
        P(),
        P(AXES, None, None),
        P(),
    )
    return jax.shard_map(
        body,
        mesh=mesh,
        in_specs=placed,
        out_specs=(P(AXES, None, None), P()),
        check_vma=False,
    )
```
